32 devices in a mesh: ray: 4 (over z), cell: 8 (over y, x, core).
Axes of the slice: x: 2, y: 2, z: 4, core: 2. Of those that a mesh axis runs over, the one named last changes fastest.
Arguments:
- right_side: float32 [8, 8192], P(None, 'ray'), may hold values from -6 to 6
- tiles: bfloat16 [32, 32, 256, 256], P('ray', 'cell'), may hold values from -0.375 to 0.375
- pattern: int32 [32, 32], P('ray', 'cell'), may hold values from 0 to 31, as said below
- counts: int32 [32, 8], P('ray', 'cell'), may hold values from 1 to 4, as said below
Outputs:
- solution: float32 [8, 65536], P(None, 'cell')
- misfit: float32 [8], replicated
The draws below stay inside these ranges and needn't reach their ends.
Inputs may be any that keep to these rules, and one draw needn't show every extreme that they name: `pattern`: each entry indexes a block within the slot's group of 32 cell blocks; a bundle may name a block more than once. Ragged counts; some bundle has all 4 slots live in some group, and some has one.
All inputs are finite; a program needn't handle non-finite values.
Results may differ from the reference program's by a relative error of at most 0.0014.
Values may be sent and summed in bfloat16 or wider, within the bound.
A program may use at most 64 MiB of HBM per device.

```python
import jax
import jax.numpy as jnp
from jax import lax

RB = 256
CB = 256
NRHS = 8
BLK_DEV = 32
KDEV = 4
ITERS = 4
SHARDS = 8
BUNDLES = 32
BLOCKS = 256
SLOTS = 32
ROWS = 8192
CELLS = 65536


def draw_pattern(key, part):
    values = jax.random.randint(jax.random.fold_in(key, 11), (BUNDLES, SLOTS), 0, BLK_DEV)
    values = values.at[0, 0].set(0).at[0, 1].set(BLK_DEV - 1)
    return values.astype(jnp.int32)


def draw_counts(key, part):
    values = jax.random.randint(jax.random.fold_in(key, 23), (BUNDLES, SHARDS), 1, KDEV + 1)
    values = values.at[0, 0].set(KDEV).at[1, 0].set(1)
    return values.astype(jnp.int32)


def shard_levels(own_key, dims, split, least, top_value):
    loudness, own = 1.0, jax.random.fold_in(own_key, 6)
    for axis_at, blocks in split:
        steps = jnp.exp(jax.random.uniform(jax.random.fold_in(own, axis_at), (blocks,), jnp.float32, least / len(split), top_value / len(split)))
        loudness = loudness * jnp.repeat(steps, dims[axis_at] // blocks).reshape([-1 if axis == axis_at else 1 for axis in range(len(dims))])
    return loudness


def noise(key, shape, scale, reach, pieces=(), kind=jnp.bfloat16):
    values = jax.random.normal(key, shape, jnp.float32) * scale
    if len(pieces) > 0:
        values = shard_levels(key, shape, pieces, -0.22, 0.18) * values
    return jnp.clip(values, min=-reach, max=reach).astype(kind)


def setup_inputs(seed: int = 0) -> dict:
    streams_of = jax.random.split(jax.random.key(seed), 5)
    right_side = noise(streams_of[0], (NRHS, ROWS), 1.0, 6.0, ((1, 4),), jnp.float32)
    tiles = noise(streams_of[1], (BUNDLES, SLOTS, RB, CB), CB ** -0.5, 0.375, ((0, 4), (1, 8)))
    pattern = draw_pattern(jax.random.fold_in(streams_of[4], 71), 0)
    counts = draw_counts(jax.random.fold_in(streams_of[4], 71), 0)
    return dict(right_side=right_side, tiles=tiles, pattern=pattern, counts=counts)


def slot_info(pattern_row, count_row):
    slot = jnp.arange(SLOTS, dtype=jnp.int32)
    group = slot // KDEV
    live = slot % KDEV < count_row[group]
    target = (group * BLK_DEV + pattern_row).astype(jnp.int32)
    return (live, target)

def forward(tiles, pattern, counts, vector):
    nrhs = vector.shape[0]
    vblocks = vector.astype(jnp.bfloat16).reshape(nrhs, BLOCKS, CB)

    def one(args):
        tile, pattern_row, count_row = args
        live, target = slot_info(pattern_row, count_row)
        picked = vblocks[:, target].astype(jnp.float32) * live[None, :, None].astype(jnp.float32)
        return jnp.einsum('src,nsc->nr', tile.astype(jnp.float32), picked)
    out = lax.map(one, (tiles, pattern, counts))
    return jnp.transpose(out, (1, 0, 2)).reshape(nrhs, ROWS)

def adjoint(tiles, pattern, counts, vector):
    nrhs = vector.shape[0]
    ublocks = jnp.transpose(vector.astype(jnp.bfloat16).reshape(nrhs, BUNDLES, RB), (1, 0, 2))

    def one(carry, args):
        tile, pattern_row, count_row, rows = args
        live, target = slot_info(pattern_row, count_row)
        per = jnp.einsum('src,nr->snc', tile.astype(jnp.float32), rows.astype(jnp.float32))
        per = per * live[:, None, None].astype(jnp.float32)
        return (carry.at[:, target].add(jnp.transpose(per, (1, 0, 2))), None)
    start = jnp.zeros((nrhs, BLOCKS, CB), jnp.float32)
    total, _ = lax.scan(one, start, (tiles, pattern, counts, ublocks))
    return total.reshape(nrhs, CELLS)

def norm_of(vector):
    return jnp.sqrt(lax.optimization_barrier(jnp.sum(vector * vector, axis=1)) + 1e-06)

def reference(right_side, tiles, pattern, counts):
    beta = norm_of(right_side)
    u = right_side / beta[:, None]
    v = adjoint(tiles, pattern, counts, u)
    alpha = norm_of(v)
    v = v / alpha[:, None]
    w = v
    x = jnp.zeros_like(v)
    phibar = beta
    rhobar = alpha
    for step in range(ITERS):
        u = forward(tiles, pattern, counts, v) - alpha[:, None] * u
        beta = norm_of(u)
        u = u / beta[:, None]
        v = adjoint(tiles, pattern, counts, u) - beta[:, None] * v
        alpha = norm_of(v)
        v = v / alpha[:, None]
        rho = jnp.sqrt(rhobar * rhobar + beta * beta)
        cosine = rhobar / rho
        sine = beta / rho
        theta = sine * alpha
        rhobar = -cosine * alpha
        phi = cosine * phibar
        phibar = sine * phibar
        x = x + (phi / rho)[:, None] * w
        w = v - (theta / rho)[:, None] * w
    return (x, phibar)
```

```python
import functools

import jax
import jax.numpy as jnp
from jax import lax
from jax.experimental import pallas as pl
from jax.experimental.pallas import tpu as pltpu
from jax.sharding import PartitionSpec as P

BLK_DEV = 32
ITERS = 4
EPS = 1e-06
F32 = jnp.float32
BF16 = jnp.bfloat16


def split(value):
    hi = value.astype(BF16)
    lo = (value - hi.astype(F32)).astype(BF16)
    return hi, lo


def wide(stat, lanes):
    return jnp.broadcast_to(stat[:, 0:1], (stat.shape[0], lanes))


def row_sum(value):
    total = jnp.sum(value, axis=1, keepdims=True)
    return jnp.broadcast_to(total, (value.shape[0], 128))


def kernel(
    R, C,
    pattern, counts, rhs, tiles_hbm,
    out, mis,
    tiles, fpart, frecv, ucat, apart, arecv, vhi, vlo, vsh, usq, vsq, cum, w, x,
    idx, prv, lst,
    tile_sem, fs, fr, us, ur, as_, ar, ns, nr, hs, hr, ls, lr, qs, qr,
):
    B, S = pattern.shape
    N = rhs.shape[0]
    RB, CB = tiles.shape[2], tiles.shape[3]
    RC = rhs.shape[1] // C
    NCH = C // B
    NB = BLK_DEV
    K = NB // R
    slots = B * S
    me_r = lax.axis_index("ray")
    me_c = lax.axis_index("cell")

    loads = []
    for b in range(B):
        load = pltpu.make_async_copy(tiles_hbm.at[b], tiles.at[b], tile_sem.at[b])
        load.start()
        loads.append(load)

    barrier = pltpu.get_barrier_semaphore()
    for d in range(1, C):
        pl.semaphore_signal(barrier, inc=1, device_id={"cell": lax.rem(me_c + d, C)}, device_id_type=pl.DeviceIdType.MESH)
    for d in range(1, R):
        pl.semaphore_signal(barrier, inc=1, device_id={"ray": lax.rem(me_r + d, R)}, device_id_type=pl.DeviceIdType.MESH)

    def remote(src, dst, send, recv, axis, peer):
        return pltpu.make_async_remote_copy(
            src_ref=src, dst_ref=dst, send_sem=send, recv_sem=recv,
            device_id={axis: peer}, device_id_type=pl.DeviceIdType.MESH,
        )

    for b in range(B):
        for s in range(S):
            idx[b * S + s] = jnp.where(s < counts[b, 0], pattern[b, s], NB)

    def chain(i, carry):
        p = idx[i]
        found = jnp.int32(slots)
        for j in range(slots):
            found = jnp.where((idx[j] == p) & (j < i), j, found)
        prv[i] = found
        return carry

    lax.fori_loop(0, slots, chain, 0)

    def final(k, carry):
        found = jnp.int32(slots)
        for j in range(slots):
            found = jnp.where(idx[j] == k, j, found)
        lst[k] = found
        return carry

    lax.fori_loop(0, NB, final, 0)

    cum[slots] = jnp.zeros((N, CB), F32)
    vhi[NB] = jnp.zeros((N, CB), BF16)
    w[...] = jnp.zeros_like(w)
    x[...] = jnp.zeros_like(x)
    vsh[...] = jnp.zeros_like(vsh)
    for j in range(C):
        hi, lo = split(rhs[:, j * RC:(j + 1) * RC])
        ucat[j, 0:N] = hi
        ucat[j, N:2 * N] = lo

    pl.semaphore_wait(barrier, (C - 1) + (R - 1))

    def ray_copies(src, dst, send, recv, d, kind):
        peer = lax.rem(me_r + d, R)
        source = lax.rem(me_r + R - d, R)
        if kind == "scatter":
            s = src.at[pl.ds(peer * K, K)]
            t = dst.at[me_r]
        elif kind == "gather":
            s = src.at[pl.ds(me_r * K, K)]
            t = dst.at[pl.ds(me_r * K, K)]
        else:
            s = src.at[me_r]
            t = dst.at[me_r]
        return remote(s, t, send.at[d], recv.at[d], "ray", peer)

    order = sorted(range(1, R), key=lambda d: abs(d - R // 2))

    def norm_start():
        sq = jnp.zeros((N, RC), F32)
        for j in range(C):
            u = ucat[j, 0:N].astype(F32) + ucat[j, N:2 * N].astype(F32)
            sq = sq + u * u
        usq[me_r] = row_sum(sq)
        copies = [ray_copies(usq, usq, ns, nr, d, "slot") for d in order]
        for copy in copies:
            copy.start()
        return copies

    def norm_end(copies):
        for copy in copies:
            copy.wait()
        total = usq[0]
        for r in range(1, R):
            total = total + usq[r]
        return jnp.sqrt(total + EPS)

    def adjoint(wait):
        for b in range(B):
            if wait:
                loads[b].wait()
            if NCH == 1:
                rows = ucat[b]
            else:
                rows = jnp.concatenate([ucat[b * NCH + h] for h in range(NCH)], axis=1)
            for s in range(S):
                i = b * S + s
                per = lax.dot_general(rows, tiles[b, s], (((1,), (0,)), ((), ())), preferred_element_type=F32)
                cum[i] = per[0:N] + per[N:2 * N] + cum[prv[i]]
        for k in range(NB):
            apart[k] = cum[lst[k]]

    def scatter():
        copies = [ray_copies(apart, arecv, as_, ar, d, "scatter") for d in order]
        for copy in copies:
            copy.start()
        arecv[me_r] = apart[pl.ds(me_r * K, K)]
        for copy in copies:
            copy.wait()

    def gather_start(beta, alpha):
        inv = wide(1.0 / beta, CB)
        back = wide(beta / alpha, CB)
        sq = jnp.zeros((N, CB), F32)
        for k in range(K):
            total = arecv[0, k]
            for r in range(1, R):
                total = total + arecv[r, k]
            v = total * inv - back * vsh[k]
            vsh[k] = v
            sq = sq + v * v
            hi, lo = split(v)
            vhi[me_r * K + k] = hi
            vlo[me_r * K + k] = lo
        vsq[me_r] = row_sum(sq)
        first = [ray_copies(vhi, vhi, hs, hr, d, "gather") for d in order]
        first += [ray_copies(vsq, vsq, qs, qr, d, "slot") for d in order]
        second = [ray_copies(vlo, vlo, ls, lr, d, "gather") for d in order]
        for copy in first + second:
            copy.start()
        return first, second

    def low_copies():
        return [ray_copies(vlo, vlo, ls, lr, d, "gather") for d in order]

    def forward(beta, cosine, sine, rho):
        group = vsq[0]
        for r in range(1, R):
            group = group + vsq[r]
        mine = me_c // NCH
        for t in range(B):
            b = lax.rem(mine + 1 + t, B)
            acc = jnp.zeros((N, RB), F32)
            for s in range(S):
                acc = acc + lax.dot_general(
                    vhi[idx[b * S + s]], tiles[b, s], (((1,), (1,)), ((), ())), preferred_element_type=F32
                )
            for h in range(NCH):
                j = b * NCH + h
                fpart[j, :, 0:RC] = acc[:, h * RC:(h + 1) * RC]
                fpart[j, :, RC:RC + 128] = group
                d = lax.rem(j - me_c + C, C)

                @pl.when(j != me_c)
                def _():
                    remote(fpart.at[j], frecv.at[me_c], fs.at[d], fr.at[d], "cell", j).start()

        frecv[me_c] = fpart[me_c]
        for d in range(1, C):
            peer = lax.rem(me_c + d, C)
            remote(fpart.at[peer], frecv.at[me_c], fs.at[d], fr.at[d], "cell", peer).wait()
        total = frecv[0]
        for j in range(1, C):
            total = total + frecv[j]
        alpha = jnp.sqrt(total[:, RC:RC + 128] + EPS)
        old = ucat[me_c, 0:N].astype(F32) + ucat[me_c, N:2 * N].astype(F32)
        u = total[:, 0:RC] * wide(1.0 / alpha, RC) - wide(alpha / beta, RC) * old
        hi, lo = split(u)
        ucat[me_c, 0:N] = hi
        ucat[me_c, N:2 * N] = lo
        copies = []
        for d in range(1, C):
            peer = lax.rem(me_c + d, C)
            copies.append(remote(ucat.at[me_c], ucat.at[me_c], us.at[d], ur.at[d], "cell", peer))
        for copy in copies:
            copy.start()
        for copy in low_copies():
            copy.wait()
        theta = sine * alpha
        rhobar = -cosine * alpha
        inv = wide(1.0 / alpha, CB)
        ratio = wide(theta / rho, CB)
        for k in range(NB):
            w[k] = (vhi[k].astype(F32) + vlo[k].astype(F32)) * inv - ratio * w[k]
        for copy in copies:
            copy.wait()
        return alpha, rhobar

    def rotate(beta, rhobar, phibar):
        rho = jnp.sqrt(rhobar * rhobar + beta * beta)
        cosine = rhobar / rho
        sine = beta / rho
        phi = cosine * phibar
        return rho, cosine, sine, sine * phibar, phi / rho

    def step_x(step):
        scale = wide(step, CB)
        for k in range(NB):
            x[k] = x[k] + scale * w[k]

    norms = norm_start()
    adjoint(True)
    scatter()
    beta = norm_end(norms)
    one = jnp.ones((N, 128), F32)
    first, _ = gather_start(beta, one)
    for copy in first:
        copy.wait()

    def body(_, carry):
        beta, cosine, sine, rho, phibar = carry
        alpha, rhobar = forward(beta, cosine, sine, rho)
        norms = norm_start()
        adjoint(False)
        scatter()
        beta = norm_end(norms)
        first, _ = gather_start(beta, alpha)
        rho, cosine, sine, phibar, step = rotate(beta, rhobar, phibar)
        step_x(step)
        for copy in first:
            copy.wait()
        return beta, cosine, sine, rho, phibar

    carry = (beta, -one, jnp.zeros((N, 128), F32), one, beta)
    beta, cosine, sine, rho, phibar = lax.fori_loop(0, ITERS - 1, body, carry)
    alpha, rhobar = forward(beta, cosine, sine, rho)
    beta = norm_end(norm_start())
    rho, cosine, sine, phibar, step = rotate(beta, rhobar, phibar)
    scale = wide(step, CB)
    for k in range(NB):
        out[:, k * CB:(k + 1) * CB] = x[k] + scale * w[k]
    mis[...] = phibar


def local(R, C, right_side, tiles, pattern, counts):
    N, rows = right_side.shape
    B, S, RB, CB = tiles.shape
    NB = BLK_DEV
    RC = rows // C
    K = NB // R
    slots = B * S
    vmem = pl.BlockSpec(memory_space=pltpu.VMEM)
    smem = pl.BlockSpec(memory_space=pltpu.SMEM)
    dma = pltpu.SemaphoreType.DMA
    x, mis = pl.pallas_call(
        functools.partial(kernel, R, C),
        out_shape=(
            jax.ShapeDtypeStruct((N, NB * CB), F32),
            jax.ShapeDtypeStruct((N, 128), F32),
        ),
        in_specs=[smem, smem, vmem, pl.BlockSpec(memory_space=pl.ANY)],
        out_specs=(vmem, vmem),
        scratch_shapes=[
            pltpu.VMEM((B, S, RB, CB), BF16),
            pltpu.VMEM((C, N, RC + 128), F32),
            pltpu.VMEM((C, N, RC + 128), F32),
            pltpu.VMEM((C, 2 * N, RC), BF16),
            pltpu.VMEM((NB, N, CB), F32),
            pltpu.VMEM((R, K, N, CB), F32),
            pltpu.VMEM((NB + 1, N, CB), BF16),
            pltpu.VMEM((NB, N, CB), BF16),
            pltpu.VMEM((K, N, CB), F32),
            pltpu.VMEM((R, N, 128), F32),
            pltpu.VMEM((R, N, 128), F32),
            pltpu.VMEM((slots + 1, N, CB), F32),
            pltpu.VMEM((NB, N, CB), F32),
            pltpu.VMEM((NB, N, CB), F32),
            pltpu.SMEM((slots,), jnp.int32),
            pltpu.SMEM((slots,), jnp.int32),
            pltpu.SMEM((NB,), jnp.int32),
            dma((B,)),
            dma((C,)), dma((C,)), dma((C,)), dma((C,)),
            dma((R,)), dma((R,)), dma((R,)), dma((R,)),
            dma((R,)), dma((R,)), dma((R,)), dma((R,)),
            dma((R,)), dma((R,)),
        ],
        compiler_params=pltpu.CompilerParams(collective_id=0, has_side_effects=True),
    )(pattern, counts, right_side, tiles)
    return x, mis[:, 0]


def solution(mesh):
    R, C = mesh.shape["ray"], mesh.shape["cell"]
    in_specs = (P(None, "ray"), P("ray", "cell", None, None), P("ray", "cell"), P("ray", "cell"))
    out_specs = (P(None, "cell"), P())
    return jax.shard_map(
        functools.partial(local, R, C), mesh=mesh, in_specs=in_specs, out_specs=out_specs, check_vma=False
    )
```

```python
import functools

import jax
import jax.numpy as jnp
from jax import lax
from jax.experimental import pallas as pl
from jax.experimental.pallas import tpu as pltpu
from jax.sharding import PartitionSpec as P

BLK_DEV = 32
ITERS = 4
PIECES = 4
EPS = 1e-06
F32 = jnp.float32
BF16 = jnp.bfloat16


def split(value):
    hi = value.astype(BF16)
    lo = (value - hi.astype(F32)).astype(BF16)
    return hi, lo


def wide(stat, lanes):
    return jnp.broadcast_to(stat[:, 0:1], (stat.shape[0], lanes))


def eye(n):
    shape = (n, 128)
    return lax.broadcasted_iota(jnp.int32, shape, 0) == lax.broadcasted_iota(jnp.int32, shape, 1)


def to_row(value):
    n = value.shape[0]
    total = jnp.broadcast_to(jnp.sum(value, axis=1, keepdims=True), (n, 128))
    return jnp.sum(jnp.where(eye(n), total, 0.0), axis=0, keepdims=True)


def wide(row, n, lanes):
    spread = jnp.where(eye(n), jnp.broadcast_to(row, (n, 128)), 0.0)
    return jnp.broadcast_to(jnp.sum(spread, axis=1, keepdims=True), (n, lanes))


def kernel(
    R, C,
    pattern_hbm, counts_hbm, rhs, tiles_hbm,
    out, mis,
    tiles, flipped, fpart, frecv, ucat, apart, arecv, vhi, vlo, vsh, usq, vsq, gsq, cum, w, x,
    pattern, counts, idx, prv, lst,
    tile_sem, small_sem, fs, fr, us, ur, as_, ar, ns, nr, hs, hr, ls, lr, qs, qr, gs, gr,
):
    S, B = pattern.shape
    N = rhs.shape[0]
    RB, CB = tiles.shape[2], tiles.shape[3]
    RC = rhs.shape[1] // C
    NCH = C // B
    NB = BLK_DEV
    K = NB // R
    pieces = min(PIECES, K)
    KP = K // pieces
    slots = B * S
    me_r = lax.axis_index("ray")
    me_c = lax.axis_index("cell")

    small = [
        pltpu.make_async_copy(pattern_hbm, pattern, small_sem.at[0]),
        pltpu.make_async_copy(counts_hbm, counts, small_sem.at[1]),
    ]
    for copy in small:
        copy.start()
    loads = []
    for b in range(B):
        load = pltpu.make_async_copy(tiles_hbm.at[b], tiles.at[b], tile_sem.at[b])
        load.start()
        loads.append(load)

    barrier = pltpu.get_barrier_semaphore()
    for d in range(1, C):
        pl.semaphore_signal(barrier, inc=1, device_id={"cell": lax.rem(me_c + d, C)}, device_id_type=pl.DeviceIdType.MESH)
    for d in range(1, R):
        pl.semaphore_signal(barrier, inc=1, device_id={"ray": lax.rem(me_r + d, R)}, device_id_type=pl.DeviceIdType.MESH)

    def remote(src, dst, send, recv, axis, peer):
        return pltpu.make_async_remote_copy(
            src_ref=src, dst_ref=dst, send_sem=send, recv_sem=recv,
            device_id={axis: peer}, device_id_type=pl.DeviceIdType.MESH,
        )

    cum[slots] = jnp.zeros((N, CB), F32)
    vhi[0, NB] = jnp.zeros((N, CB), BF16)
    vhi[1, NB] = jnp.zeros((N, CB), BF16)
    w[...] = jnp.zeros_like(w)
    x[...] = jnp.zeros_like(x)
    vsh[...] = jnp.zeros_like(vsh)
    for j in range(C):
        hi, lo = split(rhs[:, j * RC:(j + 1) * RC])
        ucat[j, 0:N] = hi
        ucat[j, N:2 * N] = lo

    for copy in small:
        copy.wait()
    for b in range(B):
        for s in range(S):
            idx[b * S + s] = jnp.where(s < counts[0, b], pattern[s, b], NB)

    def chain(i, carry):
        p = idx[i]
        found = jnp.int32(slots)
        for j in range(slots):
            found = jnp.where((idx[j] == p) & (j < i), j, found)
        prv[i] = found
        return carry

    lax.fori_loop(0, slots, chain, 0)

    def final(k, carry):
        found = jnp.int32(slots)
        for j in range(slots):
            found = jnp.where(idx[j] == k, j, found)
        lst[k] = found
        return carry

    lax.fori_loop(0, NB, final, 0)

    order = sorted(range(1, R), key=lambda d: abs(d - R // 2))

    def ray_peer(d):
        return lax.rem(me_r + d, R)

    def slot_copies(ref, send, recv):
        return [remote(ref.at[me_r], ref.at[me_r], send.at[d], recv.at[d], "ray", ray_peer(d)) for d in order]

    def cell_copies(ref, send, recv):
        return [
            remote(ref.at[me_c], ref.at[me_c], send.at[d], recv.at[d], "cell", lax.rem(me_c + d, C))
            for d in range(1, C)
        ]

    def rows_copies(ref, send, recv, start, count, p):
        own = ref.at[pl.ds(me_r * K + start, count)]
        return [remote(own, own, send.at[d, p], recv.at[d, p], "ray", ray_peer(d)) for d in order]

    def scatter_copies(p):
        return [
            remote(
                apart.at[pl.ds(ray_peer(d) * K + p * KP, KP)], arecv.at[me_r, pl.ds(p * KP, KP)],
                as_.at[d, p], ar.at[d, p], "ray", ray_peer(d),
            )
            for d in order
        ]

    def norm_start():
        sq = jnp.zeros((N, RC), F32)
        for j in range(C):
            u = ucat[j, 0:N].astype(F32) + ucat[j, N:2 * N].astype(F32)
            sq = sq + u * u
        usq[me_r] = to_row(sq)
        copies = slot_copies(usq, ns, nr)
        for copy in copies:
            copy.start()
        return copies

    def norm_end(copies):
        for copy in copies:
            copy.wait()
        total = usq[0]
        for r in range(1, R):
            total = total + usq[r]
        return jnp.sqrt(total + EPS)

    def adjoint(wait):
        for b in range(B):
            if wait:
                loads[b].wait()
            if NCH == 1:
                rows = ucat[b]
            else:
                rows = jnp.concatenate([ucat[b * NCH + h] for h in range(NCH)], axis=1)
            for s in range(S):
                i = b * S + s
                per = lax.dot_general(rows, tiles[b, s], (((1,), (0,)), ((), ())), preferred_element_type=F32)
                cum[i] = per[0:N] + per[N:2 * N] + cum[prv[i]]
        for k in range(NB):
            apart[k] = cum[lst[k]]

    def scatter_start():
        for p in range(pieces):
            for copy in scatter_copies(p):
                copy.start()
        arecv[me_r] = apart[pl.ds(me_r * K, K)]

    def gather(beta, alpha, side, beside):
        inv = wide(1.0 / beta, N, CB)
        back = wide(beta / alpha, N, CB)
        sq = jnp.zeros((N, CB), F32)
        for p in range(pieces):
            for copy in scatter_copies(p):
                copy.wait_recv()
            for k in range(p * KP, (p + 1) * KP):
                total = arecv[0, k]
                for r in range(1, R):
                    total = total + arecv[r, k]
                v = total * inv - back * vsh[k]
                vsh[k] = v
                sq = sq + v * v
                hi, lo = split(v)
                vhi[side, me_r * K + k] = hi
                vlo[side, me_r * K + k] = lo
            if p == pieces - 1:
                vsq[me_r] = to_row(sq)
                for copy in slot_copies(vsq, qs, qr):
                    copy.start()
            for copy in rows_copies(vhi.at[side], hs, hr, p * KP, KP, p):
                copy.start()
        beside()
        for p in range(pieces):
            for copy in scatter_copies(p):
                copy.wait_send()
        for copy in slot_copies(vsq, qs, qr):
            copy.wait()
        group = vsq[0]
        for r in range(1, R):
            group = group + vsq[r]
        gsq[me_c] = group
        for copy in cell_copies(gsq, gs, gr):
            copy.start()
        for p in range(pieces):
            for copy in rows_copies(vhi.at[side], hs, hr, p * KP, KP, p):
                copy.wait()
        for copy in rows_copies(vlo.at[side], ls, lr, 0, K, 0):
            copy.start()

    def forward(beta, side):
        mine = me_c // NCH
        for t in range(B):
            b = lax.rem(mine + 1 + t, B)
            acc = jnp.zeros((N, RB), F32)
            for s in range(S):
                acc = acc + lax.dot_general(
                    vhi[side, idx[b * S + s]], flipped[b, s], (((1,), (0,)), ((), ())), preferred_element_type=F32
                )
            for h in range(NCH):
                j = b * NCH + h
                fpart[j] = acc[:, h * RC:(h + 1) * RC]
                d = lax.rem(j - me_c + C, C)

                @pl.when(j != me_c)
                def _():
                    remote(fpart.at[j], frecv.at[me_c], fs.at[d], fr.at[d], "cell", j).start()

        frecv[me_c] = fpart[me_c]
        for copy in cell_copies(gsq, gs, gr):
            copy.wait()
        norm = gsq[0]
        for j in range(1, C):
            norm = norm + gsq[j]
        alpha = jnp.sqrt(norm + EPS)
        inv = wide(1.0 / alpha, N, RC)
        old = ucat[me_c, 0:N].astype(F32) + ucat[me_c, N:2 * N].astype(F32)
        old = wide(alpha / beta, N, RC) * old
        for d in range(1, C):
            peer = lax.rem(me_c + d, C)
            remote(fpart.at[peer], frecv.at[me_c], fs.at[d], fr.at[d], "cell", peer).wait()
        total = frecv[0]
        for j in range(1, C):
            total = total + frecv[j]
        hi, lo = split(total * inv - old)
        ucat[me_c, 0:N] = hi
        ucat[me_c, N:2 * N] = lo
        copies = cell_copies(ucat, us, ur)
        for copy in copies:
            copy.start()
        for copy in copies:
            copy.wait()
        return alpha

    def step_w(alpha, sine, rho, side):
        for copy in rows_copies(vlo.at[side], ls, lr, 0, K, 0):
            copy.wait()
        inv = wide(1.0 / alpha, N, CB)
        ratio = wide(sine * alpha / rho, N, CB)
        for k in range(NB):
            w[k] = (vhi[side, k].astype(F32) + vlo[side, k].astype(F32)) * inv - ratio * w[k]

    def rotate(beta, rhobar, phibar):
        rho = jnp.sqrt(rhobar * rhobar + beta * beta)
        cosine = rhobar / rho
        sine = beta / rho
        phi = cosine * phibar
        return rho, cosine, sine, sine * phibar, phi / rho

    def flip():
        def one(i, carry):
            for s in range(S):
                flipped[i, s] = tiles[i, s].T
            return carry

        lax.fori_loop(0, B, one, 0)

    adjoint(True)
    pl.semaphore_wait(barrier, (C - 1) + (R - 1))
    norms = norm_start()
    scatter_start()
    flip()
    beta = norm_end(norms)
    one = jnp.ones((1, 128), F32)
    gather(beta, one, 0, lambda: None)

    def body(step, carry):
        beta, cosine, sine, rho, phibar = carry
        side = lax.rem(step, 2)
        alpha = forward(beta, side)
        norms = norm_start()
        adjoint(False)
        scatter_start()
        step_w(alpha, sine, rho, side)
        beta = norm_end(norms)
        rho, cosine, sine, phibar, length = rotate(beta, -cosine * alpha, phibar)

        def step_x():
            scale = wide(length, N, CB)
            for k in range(NB):
                x[k] = x[k] + scale * w[k]

        gather(beta, alpha, 1 - side, step_x)
        return beta, cosine, sine, rho, phibar

    carry = (beta, -one, jnp.zeros((1, 128), F32), one, beta)
    beta, cosine, sine, rho, phibar = lax.fori_loop(0, ITERS - 1, body, carry)
    side = (ITERS - 1) % 2
    alpha = forward(beta, side)
    norms = norm_start()
    step_w(alpha, sine, rho, side)
    beta = norm_end(norms)
    rho, cosine, sine, phibar, length = rotate(beta, -cosine * alpha, phibar)
    scale = wide(length, N, CB)
    for k in range(NB):
        out[:, k * CB:(k + 1) * CB] = x[k] + scale * w[k]
    mis[...] = phibar


def local(R, C, right_side, tiles, pattern, counts):
    N, rows = right_side.shape
    B, S, RB, CB = tiles.shape
    NB = BLK_DEV
    RC = rows // C
    K = NB // R
    pieces = min(PIECES, K)
    slots = B * S
    vmem = pl.BlockSpec(memory_space=pltpu.VMEM)
    hbm = pl.BlockSpec(memory_space=pl.ANY)
    dma = pltpu.SemaphoreType.DMA
    x, mis = pl.pallas_call(
        functools.partial(kernel, R, C),
        out_shape=(
            jax.ShapeDtypeStruct((N, NB * CB), F32),
            jax.ShapeDtypeStruct((1, 128), F32),
        ),
        in_specs=[hbm, hbm, vmem, hbm],
        out_specs=(vmem, vmem),
        scratch_shapes=[
            pltpu.VMEM((B, S, RB, CB), BF16),
            pltpu.VMEM((B, S, CB, RB), BF16),
            pltpu.VMEM((C, N, RC), F32),
            pltpu.VMEM((C, N, RC), F32),
            pltpu.VMEM((C, 2 * N, RC), BF16),
            pltpu.VMEM((NB, N, CB), F32),
            pltpu.VMEM((R, K, N, CB), F32),
            pltpu.VMEM((2, NB + 1, N, CB), BF16),
            pltpu.VMEM((2, NB, N, CB), BF16),
            pltpu.VMEM((K, N, CB), F32),
            pltpu.VMEM((R, 1, 128), F32),
            pltpu.VMEM((R, 1, 128), F32),
            pltpu.VMEM((C, 1, 128), F32),
            pltpu.VMEM((slots + 1, N, CB), F32),
            pltpu.VMEM((NB, N, CB), F32),
            pltpu.VMEM((NB, N, CB), F32),
            pltpu.SMEM((S, B), jnp.int32),
            pltpu.SMEM((1, B), jnp.int32),
            pltpu.SMEM((slots,), jnp.int32),
            pltpu.SMEM((slots,), jnp.int32),
            pltpu.SMEM((NB,), jnp.int32),
            dma((B,)), dma((2,)),
            dma((C,)), dma((C,)), dma((C,)), dma((C,)),
            dma((R, pieces)), dma((R, pieces)), dma((R,)), dma((R,)),
            dma((R, pieces)), dma((R, pieces)), dma((R, 1)), dma((R, 1)),
            dma((R,)), dma((R,)), dma((C,)), dma((C,)),
        ],
        compiler_params=pltpu.CompilerParams(collective_id=0, has_side_effects=True),
    )(pattern.T, counts.T, right_side, tiles)
    return x, mis[0, :N]


def solution(mesh):
    R, C = mesh.shape["ray"], mesh.shape["cell"]
    in_specs = (P(None, "ray"), P("ray", "cell", None, None), P("ray", "cell"), P("ray", "cell"))
    out_specs = (P(None, "cell"), P())
    return jax.shard_map(
        functools.partial(local, R, C), mesh=mesh, in_specs=in_specs, out_specs=out_specs, check_vma=False
    )
```

```python
import functools

import jax
import jax.numpy as jnp
from jax import lax
from jax.experimental import pallas as pl
from jax.experimental.pallas import tpu as pltpu
from jax.sharding import PartitionSpec as P

BLK_DEV = 32
ITERS = 4
PIECES = 1
EPS = 1e-06
F32 = jnp.float32
BF16 = jnp.bfloat16


def split(value):
    hi = value.astype(BF16)
    lo = (value - hi.astype(F32)).astype(BF16)
    return hi, lo


def wide(stat, lanes):
    return jnp.broadcast_to(stat[:, 0:1], (stat.shape[0], lanes))


def eye(n):
    shape = (n, 128)
    return lax.broadcasted_iota(jnp.int32, shape, 0) == lax.broadcasted_iota(jnp.int32, shape, 1)


def to_row(value):
    n = value.shape[0]
    total = jnp.broadcast_to(jnp.sum(value, axis=1, keepdims=True), (n, 128))
    return jnp.sum(jnp.where(eye(n), total, 0.0), axis=0, keepdims=True)


def wide(row, n, lanes):
    spread = jnp.where(eye(n), jnp.broadcast_to(row, (n, 128)), 0.0)
    return jnp.broadcast_to(jnp.sum(spread, axis=1, keepdims=True), (n, lanes))


def kernel(
    R, C,
    pattern_hbm, counts_hbm, rhs, tiles_hbm,
    out, mis,
    tiles, flipped, fpart, frecv, ucat, apart, arecv, vhi, vlo, vsh, usq, vsq, gsq, cum, w, x,
    pattern, counts, idx, prv, lst,
    tile_sem, small_sem, fs, fr, us, ur, as_, ar, ns, nr, hs, hr, ls, lr, qs, qr, gs, gr,
):
    S, B = pattern.shape
    N = rhs.shape[0]
    RB, CB = tiles.shape[2], tiles.shape[3]
    RC = rhs.shape[1] // C
    NCH = C // B
    NB = BLK_DEV
    K = NB // R
    pieces = min(PIECES, K)
    KP = K // pieces
    slots = B * S
    me_r = lax.axis_index("ray")
    me_c = lax.axis_index("cell")

    small = [
        pltpu.make_async_copy(pattern_hbm, pattern, small_sem.at[0]),
        pltpu.make_async_copy(counts_hbm, counts, small_sem.at[1]),
    ]
    for copy in small:
        copy.start()
    loads = []
    for b in range(B):
        load = pltpu.make_async_copy(tiles_hbm.at[b], tiles.at[b], tile_sem.at[b])
        load.start()
        loads.append(load)

    barrier = pltpu.get_barrier_semaphore()
    for d in range(1, C):
        pl.semaphore_signal(barrier, inc=1, device_id={"cell": lax.rem(me_c + d, C)}, device_id_type=pl.DeviceIdType.MESH)
    for d in range(1, R):
        pl.semaphore_signal(barrier, inc=1, device_id={"ray": lax.rem(me_r + d, R)}, device_id_type=pl.DeviceIdType.MESH)

    def remote(src, dst, send, recv, axis, peer):
        return pltpu.make_async_remote_copy(
            src_ref=src, dst_ref=dst, send_sem=send, recv_sem=recv,
            device_id={axis: peer}, device_id_type=pl.DeviceIdType.MESH,
        )

    cum[slots] = jnp.zeros((N, CB), F32)
    vhi[0, NB] = jnp.zeros((N, CB), BF16)
    vhi[1, NB] = jnp.zeros((N, CB), BF16)
    w[...] = jnp.zeros_like(w)
    x[...] = jnp.zeros_like(x)
    vsh[...] = jnp.zeros_like(vsh)
    for j in range(C):
        hi, lo = split(rhs[:, j * RC:(j + 1) * RC])
        ucat[j, 0:N] = hi
        ucat[j, N:2 * N] = lo

    for copy in small:
        copy.wait()
    for b in range(B):
        for s in range(S):
            idx[b * S + s] = jnp.where(s < counts[0, b], pattern[s, b], NB)

    def chain(i, carry):
        p = idx[i]
        found = jnp.int32(slots)
        for j in range(slots):
            found = jnp.where((idx[j] == p) & (j < i), j, found)
        prv[i] = found
        return carry

    lax.fori_loop(0, slots, chain, 0)

    def final(k, carry):
        found = jnp.int32(slots)
        for j in range(slots):
            found = jnp.where(idx[j] == k, j, found)
        lst[k] = found
        return carry

    lax.fori_loop(0, NB, final, 0)

    order = sorted(range(1, R), key=lambda d: abs(d - R // 2))

    def ray_peer(d):
        return lax.rem(me_r + d, R)

    def slot_copies(ref, send, recv):
        return [remote(ref.at[me_r], ref.at[me_r], send.at[d], recv.at[d], "ray", ray_peer(d)) for d in order]

    def cell_copies(ref, send, recv):
        return [
            remote(ref.at[me_c], ref.at[me_c], send.at[d], recv.at[d], "cell", lax.rem(me_c + d, C))
            for d in range(1, C)
        ]

    def rows_copies(ref, send, recv, start, count, p):
        own = ref.at[pl.ds(me_r * K + start, count)]
        return [remote(own, own, send.at[d, p], recv.at[d, p], "ray", ray_peer(d)) for d in order]

    def scatter_copies(p):
        return [
            remote(
                apart.at[pl.ds(ray_peer(d) * K + p * KP, KP)], arecv.at[me_r, pl.ds(p * KP, KP)],
                as_.at[d, p], ar.at[d, p], "ray", ray_peer(d),
            )
            for d in order
        ]

    def norm_start():
        sq = jnp.zeros((N, RC), F32)
        for j in range(C):
            u = ucat[j, 0:N].astype(F32) + ucat[j, N:2 * N].astype(F32)
            sq = sq + u * u
        usq[me_r] = to_row(sq)
        copies = slot_copies(usq, ns, nr)
        for copy in copies:
            copy.start()
        return copies

    def norm_end(copies):
        for copy in copies:
            copy.wait()
        total = usq[0]
        for r in range(1, R):
            total = total + usq[r]
        return jnp.sqrt(total + EPS)

    def adjoint(wait):
        for b in range(B):
            if wait:
                loads[b].wait()
            if NCH == 1:
                rows = ucat[b]
            else:
                rows = jnp.concatenate([ucat[b * NCH + h] for h in range(NCH)], axis=1)
            for s in range(S):
                i = b * S + s
                per = lax.dot_general(rows, tiles[b, s], (((1,), (0,)), ((), ())), preferred_element_type=F32)
                cum[i] = per[0:N] + per[N:2 * N] + cum[prv[i]]
        for k in range(NB):
            apart[k] = cum[lst[k]]

    def scatter_start():
        for p in range(pieces):
            for copy in scatter_copies(p):
                copy.start()
        arecv[me_r] = apart[pl.ds(me_r * K, K)]

    def gather(beta, alpha, side, beside):
        inv = wide(1.0 / beta, N, CB)
        back = wide(beta / alpha, N, CB)
        sq = jnp.zeros((N, CB), F32)
        for p in range(pieces):
            for copy in scatter_copies(p):
                copy.wait_recv()
            for k in range(p * KP, (p + 1) * KP):
                total = arecv[0, k]
                for r in range(1, R):
                    total = total + arecv[r, k]
                v = total * inv - back * vsh[k]
                vsh[k] = v
                sq = sq + v * v
                hi, lo = split(v)
                vhi[side, me_r * K + k] = hi
                vlo[side, me_r * K + k] = lo
            if p == pieces - 1:
                vsq[me_r] = to_row(sq)
                for copy in slot_copies(vsq, qs, qr):
                    copy.start()
            for copy in rows_copies(vhi.at[side], hs, hr, p * KP, KP, p):
                copy.start()
        beside()
        for p in range(pieces):
            for copy in scatter_copies(p):
                copy.wait_send()
        for copy in slot_copies(vsq, qs, qr):
            copy.wait()
        group = vsq[0]
        for r in range(1, R):
            group = group + vsq[r]
        gsq[me_c] = group
        for copy in cell_copies(gsq, gs, gr):
            copy.start()
        for p in range(pieces):
            for copy in rows_copies(vhi.at[side], hs, hr, p * KP, KP, p):
                copy.wait()
        for copy in rows_copies(vlo.at[side], ls, lr, 0, K, 0):
            copy.start()

    def forward(beta, side):
        for b in range(B):
            acc = jnp.zeros((N, RB), F32)
            for s in range(S):
                acc = acc + lax.dot_general(
                    vhi[side, idx[b * S + s]], flipped[b, s], (((1,), (0,)), ((), ())), preferred_element_type=F32
                )
            for h in range(NCH):
                fpart[b * NCH + h] = acc[:, h * RC:(h + 1) * RC]
        for d in range(1, C):
            peer = lax.rem(me_c + d, C)
            remote(fpart.at[peer], frecv.at[me_c], fs.at[d], fr.at[d], "cell", peer).start()

        frecv[me_c] = fpart[me_c]
        for copy in cell_copies(gsq, gs, gr):
            copy.wait()
        norm = gsq[0]
        for j in range(1, C):
            norm = norm + gsq[j]
        alpha = jnp.sqrt(norm + EPS)
        inv = wide(1.0 / alpha, N, RC)
        old = ucat[me_c, 0:N].astype(F32) + ucat[me_c, N:2 * N].astype(F32)
        old = wide(alpha / beta, N, RC) * old
        for d in range(1, C):
            peer = lax.rem(me_c + d, C)
            remote(fpart.at[peer], frecv.at[me_c], fs.at[d], fr.at[d], "cell", peer).wait()
        total = frecv[0]
        for j in range(1, C):
            total = total + frecv[j]
        hi, lo = split(total * inv - old)
        ucat[me_c, 0:N] = hi
        ucat[me_c, N:2 * N] = lo
        copies = cell_copies(ucat, us, ur)
        for copy in copies:
            copy.start()
        for copy in copies:
            copy.wait()
        return alpha

    def step_w(alpha, sine, rho, side):
        for copy in rows_copies(vlo.at[side], ls, lr, 0, K, 0):
            copy.wait()
        inv = wide(1.0 / alpha, N, CB)
        ratio = wide(sine * alpha / rho, N, CB)
        for k in range(NB):
            w[k] = (vhi[side, k].astype(F32) + vlo[side, k].astype(F32)) * inv - ratio * w[k]

    def rotate(beta, rhobar, phibar):
        rho = jnp.sqrt(rhobar * rhobar + beta * beta)
        cosine = rhobar / rho
        sine = beta / rho
        phi = cosine * phibar
        return rho, cosine, sine, sine * phibar, phi / rho

    def flip():
        def one(i, carry):
            for s in range(S):
                flipped[i, s] = tiles[i, s].T
            return carry

        lax.fori_loop(0, B, one, 0)

    adjoint(True)
    pl.semaphore_wait(barrier, (C - 1) + (R - 1))
    norms = norm_start()
    scatter_start()
    flip()
    beta = norm_end(norms)
    one = jnp.ones((1, 128), F32)
    gather(beta, one, 0, lambda: None)

    def body(step, carry):
        beta, cosine, sine, rho, phibar = carry
        side = lax.rem(step, 2)
        alpha = forward(beta, side)
        norms = norm_start()
        adjoint(False)
        scatter_start()
        step_w(alpha, sine, rho, side)
        beta = norm_end(norms)
        rho, cosine, sine, phibar, length = rotate(beta, -cosine * alpha, phibar)

        def step_x():
            scale = wide(length, N, CB)
            for k in range(NB):
                x[k] = x[k] + scale * w[k]

        gather(beta, alpha, 1 - side, step_x)
        return beta, cosine, sine, rho, phibar

    carry = (beta, -one, jnp.zeros((1, 128), F32), one, beta)
    beta, cosine, sine, rho, phibar = lax.fori_loop(0, ITERS - 1, body, carry)
    side = (ITERS - 1) % 2
    alpha = forward(beta, side)
    norms = norm_start()
    step_w(alpha, sine, rho, side)
    beta = norm_end(norms)
    rho, cosine, sine, phibar, length = rotate(beta, -cosine * alpha, phibar)
    scale = wide(length, N, CB)
    for k in range(NB):
        out[:, k * CB:(k + 1) * CB] = x[k] + scale * w[k]
    mis[...] = phibar


def local(R, C, right_side, tiles, pattern, counts):
    N, rows = right_side.shape
    B, S, RB, CB = tiles.shape
    NB = BLK_DEV
    RC = rows // C
    K = NB // R
    pieces = min(PIECES, K)
    slots = B * S
    vmem = pl.BlockSpec(memory_space=pltpu.VMEM)
    hbm = pl.BlockSpec(memory_space=pl.ANY)
    dma = pltpu.SemaphoreType.DMA
    x, mis = pl.pallas_call(
        functools.partial(kernel, R, C),
        out_shape=(
            jax.ShapeDtypeStruct((N, NB * CB), F32),
            jax.ShapeDtypeStruct((1, 128), F32),
        ),
        in_specs=[hbm, hbm, vmem, hbm],
        out_specs=(vmem, vmem),
        scratch_shapes=[
            pltpu.VMEM((B, S, RB, CB), BF16),
            pltpu.VMEM((B, S, CB, RB), BF16),
            pltpu.VMEM((C, N, RC), F32),
            pltpu.VMEM((C, N, RC), F32),
            pltpu.VMEM((C, 2 * N, RC), BF16),
            pltpu.VMEM((NB, N, CB), F32),
            pltpu.VMEM((R, K, N, CB), F32),
            pltpu.VMEM((2, NB + 1, N, CB), BF16),
            pltpu.VMEM((2, NB, N, CB), BF16),
            pltpu.VMEM((K, N, CB), F32),
            pltpu.VMEM((R, 1, 128), F32),
            pltpu.VMEM((R, 1, 128), F32),
            pltpu.VMEM((C, 1, 128), F32),
            pltpu.VMEM((slots + 1, N, CB), F32),
            pltpu.VMEM((NB, N, CB), F32),
            pltpu.VMEM((NB, N, CB), F32),
            pltpu.SMEM((S, B), jnp.int32),
            pltpu.SMEM((1, B), jnp.int32),
            pltpu.SMEM((slots,), jnp.int32),
            pltpu.SMEM((slots,), jnp.int32),
            pltpu.SMEM((NB,), jnp.int32),
            dma((B,)), dma((2,)),
            dma((C,)), dma((C,)), dma((C,)), dma((C,)),
            dma((R, pieces)), dma((R, pieces)), dma((R,)), dma((R,)),
            dma((R, pieces)), dma((R, pieces)), dma((R, 1)), dma((R, 1)),
            dma((R,)), dma((R,)), dma((C,)), dma((C,)),
        ],
        compiler_params=pltpu.CompilerParams(collective_id=0, has_side_effects=True),
    )(pattern.T, counts.T, right_side, tiles)
    return x, mis[0, :N]


def solution(mesh):
    R, C = mesh.shape["ray"], mesh.shape["cell"]
    in_specs = (P(None, "ray"), P("ray", "cell", None, None), P("ray", "cell"), P("ray", "cell"))
    out_specs = (P(None, "cell"), P())
    return jax.shard_map(
        functools.partial(local, R, C), mesh=mesh, in_specs=in_specs, out_specs=out_specs, check_vma=False
    )
```
